256 devices in a mesh: blk: 64 (over y_hi, z, x), grp: 4 (over y_lo, core).
Axes of the slice: x: 4, y: 4 (y_hi: 2, y_lo: 2; y = y_hi * 2 + y_lo), z: 8, core: 2. Of those that a mesh axis runs over, the one named last changes fastest.
Arguments:
- factors: bfloat16 [2, 24576, 24576], P(None, 'blk', 'grp'), may hold values from -0.0390625 to 0.0390625
- lower_inverse: float32 [2, 24576, 128], P(None, 'blk'), may hold values from -1 to 2
- upper_inverse: float32 [2, 24576, 128], P(None, 'blk'), may hold values from -1 to 2
- right_side: float32 [2, 24576, 512], P(None, 'blk', 'grp'), may hold values from -6 to 6
Outputs:
- solution: float32 [2, 24576, 512], P(None, 'blk', 'grp')
The draws below stay inside these ranges and needn't reach their ends.
All inputs are finite; a program needn't handle non-finite values.
Results may differ from the reference program's by a relative error of at most 0.0027.
Values may be sent and summed in bfloat16 or wider, within the bound.
No kernel may reach another device: no remote copies, remote signals or barrier semaphores. Data moves between devices by JAX's collectives and lax.ppermute only.
A program may use at most 128 MiB of HBM per device.

```python
import math
import jax
import jax.numpy as jnp
from jax import lax

B = 128
ROWS_LAYER = 24576
NRHS = 512


def inverse_table(key):
    shape = (2, ROWS_LAYER, B)
    rows = lax.broadcasted_iota(jnp.int32, shape, 1) % B
    cols = lax.broadcasted_iota(jnp.int32, shape, 2)
    ident = (rows == cols).astype(jnp.float32)
    noise = 0.35 * jax.random.normal(key, shape, jnp.float32)
    return ident + noise / math.sqrt(B)


def draw_lower_inverse(key, part):
    return inverse_table(jax.random.fold_in(key, 11))


def draw_upper_inverse(key, part):
    return inverse_table(jax.random.fold_in(key, 23))


def block_levels(own_key, dims, pieces, smallest, high):
    gain, own = 1.0, jax.random.fold_in(own_key, 6)
    for position, blocks in pieces:
        draws = jnp.exp(jax.random.uniform(jax.random.fold_in(own, position), (blocks,), jnp.float32, smallest / len(pieces), high / len(pieces)))
        gain = gain * jnp.repeat(draws, dims[position] // blocks).reshape([-1 if axis == position else 1 for axis in range(len(dims))])
    return gain


def centred(stream_key, extent, spread, most, split=(), dtype=jnp.bfloat16):
    drawn = spread * jax.random.normal(stream_key, extent, jnp.float32)
    if split:
        drawn = drawn * block_levels(stream_key, extent, split, -0.22, 0.18)
    return jnp.clip(drawn, -most, most).astype(dtype)


def setup_inputs(seed: int = 0) -> dict:
    streams_of = jax.random.split(jax.random.key(seed), 5)
    return {
        "factors": centred(streams_of[0], (2, ROWS_LAYER, ROWS_LAYER), ROWS_LAYER ** -0.5, 0.0390625, ((1, 64), (2, 4))),
        "lower_inverse": draw_lower_inverse(jax.random.fold_in(streams_of[4], 71), 0),
        "upper_inverse": draw_upper_inverse(jax.random.fold_in(streams_of[4], 71), 0),
        "right_side": centred(streams_of[3], (2, ROWS_LAYER, NRHS), 1.0, 6.0, ((1, 64), (2, 4)), jnp.float32),
    }


def solve_blocks(inverse, resid):
    width = inverse.shape[1]
    count = inverse.shape[0] // width
    blocks = inverse.reshape(count, width, width)
    parts = resid.reshape(count, width, resid.shape[1])
    value = jnp.einsum("nab,nbc->nac", blocks, parts, precision=lax.Precision.HIGHEST, preferred_element_type=jnp.float32)
    return value.reshape(resid.shape)


def reference(factors, lower_inverse, upper_inverse, right_side):
    forward_first = solve_blocks(lower_inverse[0], right_side[0])
    low = forward_first.astype(jnp.bfloat16)
    coupling = jnp.dot(factors[0], low, preferred_element_type=jnp.float32)
    forward_second = solve_blocks(lower_inverse[1], right_side[1] - coupling)
    second = solve_blocks(upper_inverse[1], forward_second)
    high = second.astype(jnp.bfloat16)
    coupling = jnp.dot(factors[1], high, preferred_element_type=jnp.float32)
    first = solve_blocks(upper_inverse[0], forward_first - coupling)
    return jnp.stack([first, second])
```

```python
import jax
import jax.numpy as jnp
from jax import lax
from jax.experimental import pallas as pl
from jax.experimental.pallas import tpu as pltpu
from jax.sharding import PartitionSpec as P

INTERPRET = False
BOTH = ("blk", "grp")


def solve_blocks(inverse, resid):
    width = inverse.shape[1]
    count = inverse.shape[0] // width
    blocks = inverse.reshape(count, width, width)
    parts = resid.reshape(count, width, resid.shape[1])
    value = jnp.einsum(
        "nab,nbc->nac",
        blocks,
        parts,
        precision=lax.Precision.HIGHEST,
        preferred_element_type=jnp.float32,
    )
    return value.reshape(resid.shape)


def pairs(move):
    out = []
    for yh in range(2):
        for z in range(8):
            for x in range(4):
                for yl in range(2):
                    for c in range(2):
                        a, b, d, e, f = move(yh, z, x, yl, c)
                        out.append((((yh * 8 + z) * 4 + x) * 4 + yl * 2 + c, ((a * 8 + b) * 4 + d) * 4 + e * 2 + f))
    return out


def swap(flip):
    return pairs(lambda yh, z, x, yl, c: (yl ^ flip, c * 4 + z % 4, x, yh, z // 4))


def along_z(k):
    return pairs(lambda yh, z, x, yl, c: (yh, (z + k) % 8, x, yl, c))


def along_x(k):
    return pairs(lambda yh, z, x, yl, c: (yh, z, (x + k) % 4, yl, c))


def home(k):
    def move(yh, z, x, yl, c):
        g = (yl * 2 + c) ^ k
        return yh, z, x, g // 2, g % 2

    return pairs(move)


def send(value, perm):
    return lax.ppermute(value, BOTH, perm)


def product_kernel(place, factor, *refs):
    za = refs[0:8]
    zb = refs[8:17]
    outs = refs[17:21]
    acc = refs[21]
    rows, cols = factor.shape
    z, x, yh, grp = place[0], place[1], place[2], place[3]
    step = cols // 16
    acc[...] = jnp.zeros_like(acc)
    half = zb[7].shape[0]
    for k in range(4):
        zl = lax.rem(z - k + 8, 4)
        left, top = [], []
        for j in range(4):
            at = pl.multiple_of(zl * (4 * step) + lax.rem(x - j + 4, 4) * step, step)
            left.append(factor[:, pl.ds(at, step)])
            if k == 0:
                far = zb[7][j] if j < half else zb[8][j - half]
            else:
                far = zb[k + 3][j]
            top.append(jnp.concatenate([za[2 * j][k], za[2 * j + 1][k], zb[k][j], far], axis=1))
        value = jnp.dot(
            jnp.concatenate(left, axis=1),
            jnp.concatenate(top, axis=0),
            preferred_element_type=jnp.float32,
        )
        zh = lax.div(lax.rem(z - k + 8, 8), 4)
        n = value.shape[1] // 4
        for t in range(4):
            yl = yh if t < 2 else 1 - yh
            c = zh if t % 2 == 0 else 1 - zh
            slot = yl * 2 + c
            acc[slot] += value[:, t * n : (t + 1) * n]
    for k in range(4):
        outs[k][...] = acc[lax.bitwise_xor(grp, k)]


def product(place, factor, za, zb):
    rows, n = factor.shape[0], za[0].shape[2]
    vmem = pl.BlockSpec(memory_space=pltpu.VMEM)
    tile = jax.ShapeDtypeStruct((rows, n), jnp.float32)
    return pl.pallas_call(
        product_kernel,
        out_shape=[tile] * 4,
        in_specs=[pl.BlockSpec(memory_space=pltpu.SMEM)] + [vmem] * (1 + len(za) + len(zb)),
        out_specs=[vmem] * 4,
        scratch_shapes=[pltpu.VMEM((4, rows, n), jnp.float32)],
        interpret=INTERPRET,
    )(place, factor, *za, *zb)


def coupling_of(place, factor, piece):
    one = send(piece, swap(0))
    two = send(piece, swap(1))
    near = send(two, along_x(1))
    back = send(two, along_x(3))
    across = send(two, along_x(2))
    up = send(one, along_z(1))
    down = send(one, along_z(7))
    far = send(one, along_z(4))
    up2 = send(jnp.stack([one, up]), along_z(2))
    down2 = send(jnp.stack([down, one]), along_z(6))
    b = [jnp.stack([two, near, across, back])]
    plus, minus = b[0], b[0]
    ups, downs = [], []
    for k in range(3):
        plus = send(plus, along_z(1))
        minus = send(minus, along_z(7))
        ups.append(plus)
        downs.append(minus)
    last_up = send(plus[:2], along_z(1))
    last_down = send(minus[2:], along_z(7))
    low = jnp.concatenate([one[None], up[None], up2], axis=0)
    high = jnp.concatenate([far[None], down2, down[None]], axis=0)
    low1, high1 = send(low, along_x(1)), send(high, along_x(1))
    high3, low3 = send(high, along_x(3)), send(low, along_x(3))
    low2 = send(low1, along_x(1))
    high2 = send(high3, along_x(3))
    za = [low, high, low1, high1, low2, high2, low3, high3]
    zb = b + ups + [downs[2], downs[1], downs[0]] + [last_up, last_down]
    parts = product(place, factor, za, zb)
    total = parts[0]
    for k in range(1, 4):
        total = total + send(parts[k], home(k))
    return total


def local(factors, lower_inverse, upper_inverse, right_side):
    blk = lax.axis_index("blk")
    place = jnp.stack([blk // 4 % 8, blk % 4, blk // 32, lax.axis_index("grp")]).astype(jnp.int32)
    forward_first = solve_blocks(lower_inverse[0], right_side[0])
    coupling = coupling_of(place, factors[0], forward_first.astype(jnp.bfloat16))
    forward_second = solve_blocks(lower_inverse[1], right_side[1] - coupling)
    second = solve_blocks(upper_inverse[1], forward_second)
    coupling = coupling_of(place, factors[1], second.astype(jnp.bfloat16))
    first = solve_blocks(upper_inverse[0], forward_first - coupling)
    return jnp.stack([first, second])


def solution(mesh):
    in_specs = (
        P(None, "blk", "grp"),
        P(None, "blk", None),
        P(None, "blk", None),
        P(None, "blk", "grp"),
    )
    out_specs = P(None, "blk", "grp")
    return jax.shard_map(local, mesh=mesh, in_specs=in_specs, out_specs=out_specs, check_vma=False)
```

```python
import jax
import jax.numpy as jnp
from jax import lax
from jax.experimental import pallas as pl
from jax.experimental.pallas import tpu as pltpu
from jax.sharding import PartitionSpec as P


INTERPRET = False
VMEM = 40 * 1024 * 1024
BOTH = ("blk", "grp")


def solve_blocks(inverse, resid):
    width = inverse.shape[1]
    count = inverse.shape[0] // width
    blocks = inverse.reshape(count, width, width)
    parts = resid.reshape(count, width, resid.shape[1])
    value = jnp.einsum(
        "nab,nbc->nac",
        blocks,
        parts,
        precision=lax.Precision.HIGHEST,
        preferred_element_type=jnp.float32,
    )
    return value.reshape(resid.shape)


def pairs(move):
    out = []
    for yh in range(2):
        for z in range(8):
            for x in range(4):
                for yl in range(2):
                    for c in range(2):
                        a, b, d, e, f = move(yh, z, x, yl, c)
                        out.append((((yh * 8 + z) * 4 + x) * 4 + yl * 2 + c, ((a * 8 + b) * 4 + d) * 4 + e * 2 + f))
    return out


def swap(flip, dz, dx):
    def move(yh, z, x, yl, c):
        zh, zl = z // 4, z % 4
        return yl ^ flip, (2 * zl + c + 6 + 4 * zh + dz) % 8, (x + dx) % 4, yh, zh

    return pairs(move)


def along_z(k):
    return pairs(lambda yh, z, x, yl, c: (yh, (z + k) % 8, x, yl, c))


def along_x(k):
    return pairs(lambda yh, z, x, yl, c: (yh, z, (x + k) % 4, yl, c))


def home(k):
    def move(yh, z, x, yl, c):
        g = (yl * 2 + c) ^ k
        return yh, z, x, g // 2, g % 2

    return pairs(move)


def send(value, perm):
    return lax.ppermute(value, BOTH, perm)


LOW, HIGH = (0, 4, 1, 5), (7, 3, 2, 6)
EVEN, ODD = (0, 2), (1, 3)


def product_kernel(place, factors, *refs):
    za, zb, outs = refs[0:8], refs[8:24], refs[24:28]
    acc, factor, whole, sem = refs[28:32]
    n = acc.shape[2]
    cols = factor.shape[1]
    step = cols // 16
    layer, z, x, yh, grp = place[0], place[1], place[2], place[3], place[4]

    def fetch(zl):
        at = pl.ds(zl * (4 * step), 4 * step)
        return pltpu.make_async_copy(factors.at[layer, :, at], factor.at[:, at], sem.at[1 + zl])

    def piece(ref, k, j, yl):
        e = lax.rem(z - k + 10 + 4 * lax.rem(grp, 2), 8)
        at = pl.multiple_of(lax.rem(x - j + 4, 4) * step, step)
        lane = pl.multiple_of((2 * yl + lax.rem(e, 2)) * n, n)
        target = whole.at[lax.div(e, 2), pl.ds(at, step), pl.ds(lane, n)]
        return pltpu.make_async_copy(ref, target, sem.at[0])

    pieces = []
    for j in range(4):
        for t, ks in enumerate((LOW, HIGH)):
            for i, k in enumerate(ks):
                pieces.append((za[2 * j + t].at[i], k, j, yh))
    for k in range(8):
        for t, js in enumerate((EVEN, ODD)):
            for i, j in enumerate(js[::-1] if t and k in (4, 5) else js):
                pieces.append((zb[2 * k + t].at[i], k, j, 1 - yh))
    for args in pieces:
        piece(*args).start()
    for zl in range(4):
        fetch(zl).start()
    for args in pieces:
        piece(*args).wait()
    for zl in range(4):
        fetch(zl).wait()

    def multiply(zl, value):
        at = pl.multiple_of(zl * (4 * step), 4 * step)
        return value + jnp.dot(factor[:, pl.ds(at, 4 * step)], whole[zl], preferred_element_type=jnp.float32)

    value = lax.fori_loop(0, 4, multiply, jnp.zeros((factor.shape[0], 4 * n), jnp.float32))
    for s in range(4):
        acc[s] = value[:, s * n : (s + 1) * n]
    for k in range(4):
        outs[k][...] = acc[lax.bitwise_xor(grp, k)]


def product(place, factors, za, zb):
    _, rows, cols = factors.shape
    n = za[0].shape[2]
    anywhere = pl.BlockSpec(memory_space=pl.ANY)
    vmem = pl.BlockSpec(memory_space=pltpu.VMEM)
    tile = jax.ShapeDtypeStruct((rows, n), jnp.float32)
    return pl.pallas_call(
        product_kernel,
        out_shape=[tile] * 4,
        in_specs=[pl.BlockSpec(memory_space=pltpu.SMEM), anywhere] + [vmem] * (len(za) + len(zb)),
        out_specs=[vmem] * 4,
        scratch_shapes=[
            pltpu.VMEM((4, rows, n), jnp.float32),
            pltpu.VMEM((rows, cols), jnp.bfloat16),
            pltpu.VMEM((4, cols // 4, 4 * n), jnp.bfloat16),
            pltpu.SemaphoreType.DMA((5,)),
        ],
        compiler_params=pltpu.CompilerParams(vmem_limit_bytes=VMEM),
        interpret=INTERPRET,
    )(place, factors, *za, *zb)


def coupling_of(place, factors, piece):
    two = jnp.stack([send(piece, swap(1, 0, 0)), send(piece, swap(1, 0, 2))])
    one = jnp.stack([send(piece, swap(0, 0, 0)), send(piece, swap(0, 4, 0))])
    even, odd = [two] + [None] * 7, [send(two, along_x(1))] + [None] * 7
    for k in range(1, 4):
        for name, rows in (("e", even), ("o", odd)):
            if name == "o" and k == 3:
                break
            rows[k] = send(rows[k - 1], along_z(1))
            rows[8 - k] = send(rows[(9 - k) % 8], along_z(7))
    even[4] = send(even[3], along_z(1))
    odd[3] = send(even[3], along_x(1))
    odd[5] = send(even[5], along_x(3))
    odd[4] = send(even[4], along_x(3))
    up, down = send(one, along_z(1)), send(one, along_z(7))
    up2 = send(up, along_z(1))
    low, high = jnp.concatenate([one, up]), jnp.concatenate([down, up2])
    low1, low3 = send(low, along_x(1)), send(low, along_x(3))
    high1, high3 = send(high, along_x(1)), send(high, along_x(3))
    low2 = send(low1, along_x(1))
    high2 = send(high3, along_x(3))
    za = [low, high, low1, high1, low2, high2, low3, high3]
    zb = [row for pair in zip(even, odd) for row in pair]
    parts = product(place, factors, za, zb)
    total = parts[0]
    for k in (3, 2, 1):
        total = total + send(parts[k], home(k))
    return total


def local(factors, lower_inverse, upper_inverse, right_side):
    blk = lax.axis_index("blk")

    def place(layer):
        return jnp.stack([layer, blk // 4 % 8, blk % 4, blk // 32, lax.axis_index("grp")]).astype(jnp.int32)

    forward_first = solve_blocks(lower_inverse[0], right_side[0])
    coupling = coupling_of(place(0), factors, forward_first.astype(jnp.bfloat16))
    forward_second = solve_blocks(lower_inverse[1], right_side[1] - coupling)
    second = solve_blocks(upper_inverse[1], forward_second)
    coupling = coupling_of(place(1), factors, second.astype(jnp.bfloat16))
    first = solve_blocks(upper_inverse[0], forward_first - coupling)
    return jnp.stack([first, second])


def solution(mesh):
    in_specs = (
        P(None, "blk", "grp"),
        P(None, "blk", None),
        P(None, "blk", None),
        P(None, "blk", "grp"),
    )
    out_specs = P(None, "blk", "grp")
    return jax.shard_map(local, mesh=mesh, in_specs=in_specs, out_specs=out_specs, check_vma=False)
```

```python
import jax
import jax.numpy as jnp
from jax import lax
from jax.experimental import pallas as pl
from jax.experimental.pallas import tpu as pltpu
from jax.sharding import PartitionSpec as P


INTERPRET = False
VMEM = 58 * 1024 * 1024
BOTH = ("blk", "grp")


def solve_blocks(inverse, resid):
    width = inverse.shape[1]
    count = inverse.shape[0] // width
    blocks = inverse.reshape(count, width, width)
    parts = resid.reshape(count, width, resid.shape[1])
    value = jnp.einsum(
        "nab,nbc->nac",
        blocks,
        parts,
        precision=lax.Precision.HIGHEST,
        preferred_element_type=jnp.float32,
    )
    return value.reshape(resid.shape)


def pairs(move):
    out = []
    for yh in range(2):
        for z in range(8):
            for x in range(4):
                for yl in range(2):
                    for c in range(2):
                        a, b, d, e, f = move(yh, z, x, yl, c)
                        out.append((((yh * 8 + z) * 4 + x) * 4 + yl * 2 + c, ((a * 8 + b) * 4 + d) * 4 + e * 2 + f))
    return out


def swap(flip, dz, dx):
    def move(yh, z, x, yl, c):
        zh, zl = z // 4, z % 4
        return yl ^ flip, (2 * zl + c + 6 + 4 * zh + dz) % 8, (x + dx) % 4, yh, zh

    return pairs(move)


def along_z(k):
    return pairs(lambda yh, z, x, yl, c: (yh, (z + k) % 8, x, yl, c))


def along_x(k):
    return pairs(lambda yh, z, x, yl, c: (yh, z, (x + k) % 4, yl, c))


def home(k):
    def move(yh, z, x, yl, c):
        g = (yl * 2 + c) ^ k
        return yh, z, x, g // 2, g % 2

    return pairs(move)


def send(value, perm):
    return lax.ppermute(value, BOTH, perm)


LOW, HIGH = (0, 4, 1, 5), (7, 3, 2, 6)
EVEN, ODD = (0, 2), (1, 3)


def product_kernel(place, factors, *refs):
    za, zb, outs = refs[0:8], refs[8:24], refs[24:28]
    acc, factor, whole, sem = refs[28:32]
    n = acc.shape[2]
    cols = factor.shape[1]
    step = cols // 16
    layer, z, x, yh, grp = place[0], place[1], place[2], place[3], place[4]

    def fetch(zl):
        at = pl.ds(zl * (4 * step), 4 * step)
        return pltpu.make_async_copy(factors.at[layer, :, at], factor.at[:, at], sem.at[1 + zl])

    def piece(ref, k, j, yl):
        e = lax.rem(z - k + 10 + 4 * lax.rem(grp, 2), 8)
        at = pl.multiple_of(lax.rem(x - j + 4, 4) * step, step)
        lane = pl.multiple_of((2 * yl + lax.rem(e, 2)) * n, n)
        target = whole.at[lax.div(e, 2), pl.ds(at, step), pl.ds(lane, n)]
        return pltpu.make_async_copy(ref, target, sem.at[0])

    pieces = []
    for j in range(4):
        for t, ks in enumerate((LOW, HIGH)):
            for i, k in enumerate(ks):
                pieces.append((za[2 * j + t].at[i], k, j, yh))
    for k in range(8):
        for t, js in enumerate((EVEN, ODD)):
            for i, j in enumerate(js):
                pieces.append((zb[2 * k + t].at[i], k, j, 1 - yh))
    for args in pieces:
        piece(*args).start()
    for zl in range(4):
        fetch(zl).start()
    for args in pieces:
        piece(*args).wait()
    for zl in range(4):
        fetch(zl).wait()

    def multiply(zl, value):
        at = pl.multiple_of(zl * (4 * step), 4 * step)
        return value + jnp.dot(factor[:, pl.ds(at, 4 * step)], whole[zl], preferred_element_type=jnp.float32)

    value = lax.fori_loop(0, 4, multiply, jnp.zeros((factor.shape[0], 4 * n), jnp.float32))
    for s in range(4):
        acc[s] = value[:, s * n : (s + 1) * n]
    for k in range(4):
        outs[k][...] = acc[lax.bitwise_xor(grp, k)]


def product(place, factors, za, zb):
    _, rows, cols = factors.shape
    n = za[0].shape[2]
    anywhere = pl.BlockSpec(memory_space=pl.ANY)
    vmem = pl.BlockSpec(memory_space=pltpu.VMEM)
    tile = jax.ShapeDtypeStruct((rows, n), jnp.float32)
    return pl.pallas_call(
        product_kernel,
        out_shape=[tile] * 4,
        in_specs=[pl.BlockSpec(memory_space=pltpu.SMEM)] + [anywhere] * (1 + len(za) + len(zb)),
        out_specs=[vmem] * 4,
        scratch_shapes=[
            pltpu.VMEM((4, rows, n), jnp.float32),
            pltpu.VMEM((rows, cols), jnp.bfloat16),
            pltpu.VMEM((4, cols // 4, 4 * n), jnp.bfloat16),
            pltpu.SemaphoreType.DMA((5,)),
        ],
        compiler_params=pltpu.CompilerParams(vmem_limit_bytes=VMEM),
        interpret=INTERPRET,
    )(place, factors, *za, *zb)


def coupling_of(place, factors, piece):
    two = jnp.stack([send(piece, swap(1, 0, 0)), send(piece, swap(1, 0, 2))])
    one = jnp.stack([send(piece, swap(0, 0, 0)), send(piece, swap(0, 4, 0))])
    even, odd = [two] + [None] * 7, [send(two, along_x(1))] + [None] * 7
    for k in range(1, 4):
        for rows in (even, odd):
            rows[k] = send(rows[k - 1], along_z(1))
            rows[8 - k] = send(rows[(9 - k) % 8], along_z(7))
    even[4] = send(even[3], along_z(1))
    odd[4] = send(odd[5], along_z(7))
    up, down = send(one, along_z(1)), send(one, along_z(7))
    up2 = send(up, along_z(1))
    low, high = jnp.concatenate([one, up]), jnp.concatenate([down, up2])
    low1, low3 = send(low, along_x(1)), send(low, along_x(3))
    high1, high3 = send(high, along_x(1)), send(high, along_x(3))
    low2 = send(low1, along_x(1))
    high2 = send(high3, along_x(3))
    za = [low, high, low1, high1, low2, high2, low3, high3]
    zb = [row for pair in zip(even, odd) for row in pair]
    parts = product(place, factors, za, zb)
    total = parts[0]
    for k in (3, 2, 1):
        total = total + send(parts[k], home(k))
    return total


def local(factors, lower_inverse, upper_inverse, right_side):
    blk = lax.axis_index("blk")
    forward_first = solve_blocks(lower_inverse[0], right_side[0])
    resid = jnp.stack([right_side[1], forward_first])

    def sweep(layer, carry):
        piece, _, last = carry
        place = jnp.stack([layer, blk // 4 % 8, blk % 4, blk // 32, lax.axis_index("grp")]).astype(jnp.int32)
        value = resid[layer] - coupling_of(place, factors, piece)
        forward = solve_blocks(lower_inverse[1], value)
        value = jnp.where(layer == 0, forward, value)
        value = solve_blocks(upper_inverse[1 - layer], value)
        return value.astype(jnp.bfloat16), last, value

    start = (forward_first.astype(jnp.bfloat16), forward_first, forward_first)
    _, second, first = lax.fori_loop(0, 2, sweep, start)
    return jnp.stack([first, second])


def solution(mesh):
    in_specs = (
        P(None, "blk", "grp"),
        P(None, "blk", None),
        P(None, "blk", None),
        P(None, "blk", "grp"),
    )
    out_specs = P(None, "blk", "grp")
    return jax.shard_map(local, mesh=mesh, in_specs=in_specs, out_specs=out_specs, check_vma=False)
```

```python
import functools

import jax
import jax.numpy as jnp
from jax import lax
from jax.experimental import pallas as pl
from jax.experimental.pallas import tpu as pltpu
from jax.sharding import PartitionSpec as P


INTERPRET = False
VMEM = 58 * 1024 * 1024
BOTH = ("blk", "grp")


def solve_blocks(inverse, resid):
    width = inverse.shape[1]
    count = inverse.shape[0] // width
    blocks = inverse.reshape(count, width, width)
    parts = resid.reshape(count, width, resid.shape[1])
    value = jnp.einsum(
        "nab,nbc->nac",
        blocks,
        parts,
        precision=lax.Precision.HIGHEST,
        preferred_element_type=jnp.float32,
    )
    return value.reshape(resid.shape)


def pairs(move):
    out = []
    for yh in range(2):
        for z in range(8):
            for x in range(4):
                for yl in range(2):
                    for c in range(2):
                        a, b, d, e, f = move(yh, z, x, yl, c)
                        out.append((((yh * 8 + z) * 4 + x) * 4 + yl * 2 + c, ((a * 8 + b) * 4 + d) * 4 + e * 2 + f))
    return out


def swap(flip, dz, dx):
    def move(yh, z, x, yl, c):
        zh, zl = z // 4, z % 4
        return yl ^ flip, (2 * zl + c + 6 + 4 * zh + dz) % 8, (x + dx) % 4, yh, zh

    return pairs(move)


def along_z(k):
    return pairs(lambda yh, z, x, yl, c: (yh, (z + k) % 8, x, yl, c))


def along_x(k):
    return pairs(lambda yh, z, x, yl, c: (yh, z, (x + k) % 4, yl, c))


def home(k):
    def move(yh, z, x, yl, c):
        g = (yl * 2 + c) ^ k
        return yh, z, x, g // 2, g % 2

    return pairs(move)


def send(value, perm):
    return lax.ppermute(value, BOTH, perm)


LOW, HIGH = (0, 4, 1, 5), (7, 3, 2, 6)
EVEN, ODD = (0, 2), (1, 3)


def product_kernel(place, sweep, factors, *refs, home_half):
    za, zb, outs = refs[0:8], refs[8:24], refs[24:26]
    acc, factor, whole, sem = refs[26:30]
    n = acc.shape[2]
    cols = factor.shape[1]
    step = cols // 16
    layer, z, x, yh, grp = sweep[0], place[0], place[1], place[2], place[3]
    core = lax.rem(grp, 2)
    wanted = lax.div(grp, 2) if home_half else 1 - lax.div(grp, 2)

    def turn(k):
        return lax.rem(z - k + 10 + 4 * core, 8)

    def visit(v):
        return lax.rem(lax.div(turn(0), 2) + jnp.where(v == 1, 3, jnp.where(v == 0, 0, v - 1)), 4)

    def fetch(v):
        at = pl.ds(pl.multiple_of(visit(v) * (4 * step), 4 * step), 4 * step)
        return pltpu.make_async_copy(factors.at[layer, :, at], factor.at[:, at], sem.at[4 + v])

    def piece(ref, k, j):
        e = turn(k)
        at = pl.multiple_of(lax.rem(x - j + 4, 4) * step, step)
        lane = pl.multiple_of(lax.rem(e, 2) * n, n)
        target = whole.at[lax.div(e, 2), pl.ds(at, step), pl.ds(lane, n)]
        pltpu.make_async_copy(ref, target, sem.at[lax.div(e, 2)]).start()

    fetch(0).start()
    order = (0, 1, 7, 2, 6, 3, 5, 4)

    @pl.when(wanted == yh)
    def _():
        for k in order:
            t, ks = (0, LOW) if k in LOW else (1, HIGH)
            for j in range(4):
                piece(za[2 * j + t].at[ks.index(k)], k, j)

    @pl.when(wanted != yh)
    def _():
        for k in order:
            for t, js in enumerate((EVEN, ODD)):
                for i, j in enumerate(js):
                    piece(zb[2 * k + t].at[i], k, j)

    for v in range(1, 4):
        fetch(v).start()

    def multiply(v, value):
        zl = visit(v)
        fetch(v).wait()
        pltpu.make_async_copy(whole.at[zl], whole.at[zl], sem.at[zl]).wait()
        at = pl.multiple_of(zl * (4 * step), 4 * step)
        return value + jnp.dot(factor[:, pl.ds(at, 4 * step)], whole[zl], preferred_element_type=jnp.float32)

    value = lax.fori_loop(0, 4, multiply, jnp.zeros((factor.shape[0], 2 * n), jnp.float32))
    for s in range(2):
        acc[s] = value[:, s * n : (s + 1) * n]
    outs[0][...] = acc[core]
    outs[1][...] = acc[1 - core]


def product(place, layer, factors, za, zb, home_half):
    _, rows, cols = factors.shape
    n = za[0].shape[2]
    anywhere = pl.BlockSpec(memory_space=pl.ANY)
    vmem = pl.BlockSpec(memory_space=pltpu.VMEM)
    tile = jax.ShapeDtypeStruct((rows, n), jnp.float32)
    return pl.pallas_call(
        functools.partial(product_kernel, home_half=home_half),
        out_shape=[tile] * 2,
        in_specs=[pl.BlockSpec(memory_space=pltpu.SMEM)] * 2 + [anywhere] * (1 + len(za) + len(zb)),
        out_specs=[vmem] * 2,
        scratch_shapes=[
            pltpu.VMEM((2, rows, n), jnp.float32),
            pltpu.VMEM((rows, cols), jnp.bfloat16),
            pltpu.VMEM((4, cols // 4, 2 * n), jnp.bfloat16),
            pltpu.SemaphoreType.DMA((8,)),
        ],
        compiler_params=pltpu.CompilerParams(vmem_limit_bytes=VMEM),
        interpret=INTERPRET,
    )(place, layer.reshape(1), factors, *za, *zb)


def coupling_of(place, layer, factors, piece):
    two = jnp.stack([send(piece, swap(1, 0, 0)), send(piece, swap(1, 0, 2))])
    one = jnp.stack([send(piece, swap(0, 0, 0)), send(piece, swap(0, 4, 0))])
    even, odd = [two] + [None] * 7, [send(two, along_x(1))] + [None] * 7
    for k in range(1, 4):
        for rows in (even, odd):
            rows[k] = send(rows[k - 1], along_z(1))
            rows[8 - k] = send(rows[(9 - k) % 8], along_z(7))
    even[4] = send(even[3], along_z(1))
    odd[4] = send(odd[5], along_z(7))
    up, down = send(one, along_z(1)), send(one, along_z(7))
    up2 = send(up, along_z(1))
    low, high = jnp.concatenate([one, up]), jnp.concatenate([down, up2])
    low1, low3 = send(low, along_x(1)), send(low, along_x(3))
    high1, high3 = send(high, along_x(1)), send(high, along_x(3))
    low2 = send(low1, along_x(1))
    high2 = send(high3, along_x(3))
    za = [low, high, low1, high1, low2, high2, low3, high3]
    zb = [row for pair in zip(even, odd) for row in pair]
    away, beyond = product(place, layer, factors, za, zb, False)
    beyond, away = send(beyond, home(3)), send(away, home(2))
    near, partner = product(place, layer, factors, za, zb, True)
    total = near + send(partner, home(1)) + beyond + away
    return total


def local(factors, lower_inverse, upper_inverse, right_side):
    blk = lax.axis_index("blk")
    place = jnp.stack([blk // 4 % 8, blk % 4, blk // 32, lax.axis_index("grp")]).astype(jnp.int32)
    forward_first = solve_blocks(lower_inverse[0], right_side[0])

    def sweep(layer, carry):
        piece, out = carry
        coupling = coupling_of(place, layer, factors, piece)
        value = jnp.where(layer == 0, right_side[1], forward_first) - coupling
        forward = solve_blocks(lower_inverse[1], value)
        value = jnp.where(layer == 0, forward, value)
        value = solve_blocks(upper_inverse[1 - layer], value)
        return value.astype(jnp.bfloat16), lax.dynamic_update_index_in_dim(out, value, 1 - layer, 0)

    start = (forward_first.astype(jnp.bfloat16), jnp.zeros_like(right_side))
    return lax.fori_loop(0, 2, sweep, start)[1]


def solution(mesh):
    in_specs = (
        P(None, "blk", "grp"),
        P(None, "blk", None),
        P(None, "blk", None),
        P(None, "blk", "grp"),
    )
    out_specs = P(None, "blk", "grp")
    return jax.shard_map(local, mesh=mesh, in_specs=in_specs, out_specs=out_specs, check_vma=False)
```

```python
import functools

import jax
import jax.numpy as jnp
from jax import lax
from jax.experimental import pallas as pl
from jax.experimental.pallas import tpu as pltpu
from jax.sharding import PartitionSpec as P


INTERPRET = False
VMEM = 58 * 1024 * 1024
BOTH = ("blk", "grp")


def solve_blocks(inverse, resid):
    width = inverse.shape[1]
    count = inverse.shape[0] // width
    blocks = inverse.reshape(count, width, width)
    parts = resid.reshape(count, width, resid.shape[1])
    value = jnp.einsum(
        "nab,nbc->nac",
        blocks,
        parts,
        precision=lax.Precision.HIGHEST,
        preferred_element_type=jnp.float32,
    )
    return value.reshape(resid.shape)


def pairs(move):
    out = []
    for yh in range(2):
        for z in range(8):
            for x in range(4):
                for yl in range(2):
                    for c in range(2):
                        a, b, d, e, f = move(yh, z, x, yl, c)
                        out.append((((yh * 8 + z) * 4 + x) * 4 + yl * 2 + c, ((a * 8 + b) * 4 + d) * 4 + e * 2 + f))
    return out


def swap(flip, dz, dx):
    def move(yh, z, x, yl, c):
        zh, zl = z // 4, z % 4
        return yl ^ flip, (2 * zl + c + 6 + 4 * zh + dz) % 8, (x + dx) % 4, yh, zh

    return pairs(move)


def along_z(k):
    return pairs(lambda yh, z, x, yl, c: (yh, (z + k) % 8, x, yl, c))


def along_x(k):
    return pairs(lambda yh, z, x, yl, c: (yh, z, (x + k) % 4, yl, c))


def home(k):
    def move(yh, z, x, yl, c):
        g = (yl * 2 + c) ^ k
        return yh, z, x, g // 2, g % 2

    return pairs(move)


def send(value, perm):
    return lax.ppermute(value, BOTH, perm)


LOW, HIGH = (0, 4, 1, 5), (7, 3, 2, 6)
EVEN, ODD = (0, 2), (1, 3)


def product_kernel(place, sweep, factors, *refs, home_half):
    za, zb, outs = refs[0:8], refs[8:24], refs[24:26]
    acc, factor, whole, sem = refs[26:30]
    n = acc.shape[2]
    cols = factor.shape[1]
    step = cols // 16
    layer, z, x, yh, grp = sweep[0], place[0], place[1], place[2], place[3]
    core = lax.rem(grp, 2)
    wanted = lax.div(grp, 2) if home_half else 1 - lax.div(grp, 2)

    def turn(k):
        return lax.rem(z - k + 10 + 4 * core, 8)

    def visit(v):
        return lax.rem(lax.div(turn(0), 2) + jnp.where(v == 1, 3, jnp.where(v == 0, 0, v - 1)), 4)

    def fetch(v):
        at = pl.ds(pl.multiple_of(visit(v) * (4 * step), 4 * step), 4 * step)
        return pltpu.make_async_copy(factors.at[layer, :, at], factor.at[:, at], sem.at[4 + v])

    def piece(ref, k, j):
        e = turn(k)
        at = pl.multiple_of(lax.rem(x - j + 4, 4) * step, step)
        lane = pl.multiple_of(lax.rem(e, 2) * n, n)
        target = whole.at[lax.div(e, 2), pl.ds(at, step), pl.ds(lane, n)]
        pltpu.make_async_copy(ref, target, sem.at[lax.div(e, 2)]).start()

    fetch(0).start()
    order = (0, 1, 7, 2, 6, 3, 5, 4)

    @pl.when(wanted == yh)
    def _():
        for k in order:
            t, ks = (0, LOW) if k in LOW else (1, HIGH)
            for j in range(4):
                piece(za[2 * j + t].at[ks.index(k)], k, j)

    @pl.when(wanted != yh)
    def _():
        for k in order:
            for t, js in enumerate((EVEN, ODD)):
                for i, j in enumerate(js[::-1] if t and k > 3 else js):
                    piece(zb[2 * k + t].at[i], k, j)

    for v in range(1, 4):
        fetch(v).start()

    def multiply(v, value):
        zl = visit(v)
        fetch(v).wait()
        pltpu.make_async_copy(whole.at[zl], whole.at[zl], sem.at[zl]).wait()
        at = pl.multiple_of(zl * (4 * step), 4 * step)
        return value + jnp.dot(factor[:, pl.ds(at, 4 * step)], whole[zl], preferred_element_type=jnp.float32)

    value = lax.fori_loop(0, 4, multiply, jnp.zeros((factor.shape[0], 2 * n), jnp.float32))
    for s in range(2):
        acc[s] = value[:, s * n : (s + 1) * n]
    outs[0][...] = acc[core]
    outs[1][...] = acc[1 - core]


def product(place, layer, factors, za, zb, home_half):
    _, rows, cols = factors.shape
    n = za[0].shape[2]
    anywhere = pl.BlockSpec(memory_space=pl.ANY)
    vmem = pl.BlockSpec(memory_space=pltpu.VMEM)
    tile = jax.ShapeDtypeStruct((rows, n), jnp.float32)
    return pl.pallas_call(
        functools.partial(product_kernel, home_half=home_half),
        out_shape=[tile] * 2,
        in_specs=[pl.BlockSpec(memory_space=pltpu.SMEM)] * 2 + [anywhere] * (1 + len(za) + len(zb)),
        out_specs=[vmem] * 2,
        scratch_shapes=[
            pltpu.VMEM((2, rows, n), jnp.float32),
            pltpu.VMEM((rows, cols), jnp.bfloat16),
            pltpu.VMEM((4, cols // 4, 2 * n), jnp.bfloat16),
            pltpu.SemaphoreType.DMA((8,)),
        ],
        compiler_params=pltpu.CompilerParams(vmem_limit_bytes=VMEM),
        interpret=INTERPRET,
    )(place, layer.reshape(1), factors, *za, *zb)


def coupling_of(place, layer, factors, piece):
    two = jnp.stack([send(piece, swap(1, 0, 0)), send(piece, swap(1, 0, 2))])
    one = jnp.stack([send(piece, swap(0, 0, 0)), send(piece, swap(0, 4, 0))])
    even, odd = [two] + [None] * 7, [send(two, along_x(1))] + [None] * 7
    for k in range(1, 4):
        for name, rows in (("e", even), ("o", odd)):
            if name == "o" and k == 1:
                rows[1], rows[7] = send(even[1], along_x(1)), send(even[7], along_x(3))
                continue
            rows[k] = send(rows[k - 1], along_z(1))
            rows[8 - k] = send(rows[(9 - k) % 8], along_z(7))
    even[4] = send(even[3], along_z(1))
    odd[4] = send(odd[5], along_z(7))
    up, down = send(one, along_z(1)), send(one, along_z(7))
    up2 = send(up, along_z(1))
    low, high = jnp.concatenate([one, up]), jnp.concatenate([down, up2])
    low1, low3 = send(low, along_x(1)), send(low, along_x(3))
    high1, high3 = send(high, along_x(1)), send(high, along_x(3))
    low2 = send(low1, along_x(1))
    high2 = send(high3, along_x(3))
    za = [low, high, low1, high1, low2, high2, low3, high3]
    zb = [row for pair in zip(even, odd) for row in pair]
    away, beyond = product(place, layer, factors, za, zb, False)
    beyond, away = send(beyond, home(3)), send(away, home(2))
    near, partner = product(place, layer, factors, za, zb, True)
    total = near + send(partner, home(1)) + beyond + away
    return total


def local(factors, lower_inverse, upper_inverse, right_side):
    blk = lax.axis_index("blk")
    place = jnp.stack([blk // 4 % 8, blk % 4, blk // 32, lax.axis_index("grp")]).astype(jnp.int32)
    forward_first = solve_blocks(lower_inverse[0], right_side[0])

    def sweep(layer, carry):
        piece, out = carry
        coupling = coupling_of(place, layer, factors, piece)
        value = jnp.where(layer == 0, right_side[1], forward_first) - coupling
        forward = solve_blocks(lower_inverse[1], value)
        value = jnp.where(layer == 0, forward, value)
        value = solve_blocks(upper_inverse[1 - layer], value)
        return value.astype(jnp.bfloat16), lax.dynamic_update_index_in_dim(out, value, 1 - layer, 0)

    start = (forward_first.astype(jnp.bfloat16), jnp.zeros_like(right_side))
    return lax.fori_loop(0, 2, sweep, start)[1]


def solution(mesh):
    in_specs = (
        P(None, "blk", "grp"),
        P(None, "blk", None),
        P(None, "blk", None),
        P(None, "blk", "grp"),
    )
    out_specs = P(None, "blk", "grp")
    return jax.shard_map(local, mesh=mesh, in_specs=in_specs, out_specs=out_specs, check_vma=False)
```
